32 devices in a mesh: grp: 2 (over x), span: 16 (over z, y, core).
Axes of the slice: x: 2, y: 2, z: 4, core: 2. Of those that a mesh axis runs over, the one named last changes fastest.
Arguments:
- first_exposure: bfloat16 [1920, 96, 192], P(('grp', 'span')), parts along dimension 0, may hold values from 0 to 30
- second_exposure: bfloat16 [1920, 96, 192], P(('grp', 'span')), parts along dimension 0, may hold values from 0 to 30
- windows: int32 [256], P(('grp', 'span')), parts along dimension 0, may hold values from 0 to 10239, as said below
- shifts: int32 [3, 256], P(None, ('grp', 'span')), parts along dimension 1, may hold values from -8 to 8, as said below
Outputs:
- smoothed_update: float32 [3, 160, 128], P(None, ('grp', 'span')), parts along dimension 1
The draws below stay inside these ranges and needn't reach their ends.
There are 2 independent parts, one for each index of `grp`. The reference program is written for one: setup_inputs(seed, part) draws one part's arguments, and reference() takes and returns one part's arrays. A program takes and returns all parts, laid end to end along the dimension named above; each array names one. Nothing has to cross between parts.
Inputs may be any that keep to these rules, and one draw needn't show every extreme that they name: The windows of one device are distinct nodes whose spanwise grid row j has j // 5 equal to that device's index along span; exactly 4 of them have j % 5 < 2. `shifts`: row 0 is the spanwise shift (at most 3 in size), row 1 the wall-normal one (at most 4 in size), row 2 the streamwise one (at most 8 in size).
All inputs are finite; a program needn't handle non-finite values.
Results may differ from the reference program's by a relative error of at most 0.0022.
Values may be sent and summed in bfloat16 or wider, within the bound.
A program may use at most 128 MiB of HBM per device.

```python
import jax
import jax.numpy as jnp
from jax import lax

W = 48
STRIDE = 12
CY = 60
NZ = 96
NX = 192
WIN_DEV = 8
DYM = 3
DZM = 4
DXM = 8
CAP = 4
NY = 960
GY = 80
GZ = 8
GX = 16
GZX = 128
WINDOWS = 128


def field_plan(key):
    base = jax.random.fold_in(key, 6173)
    keys = jax.random.split(base, 4)
    span_base = jax.random.randint(keys[0], (GY, 1, 1), -DYM, DYM + 1, dtype=jnp.int32)
    deep_base = jax.random.randint(keys[1], (GY, 1, 1), -DZM, DZM + 1, dtype=jnp.int32)
    along_base = jax.random.randint(keys[2], (GY, GZ, 1), -DXM, DXM + 1, dtype=jnp.int32)
    jitter = jax.random.randint(keys[3], (3, GY, GZ, GX), -1, 2, dtype=jnp.int32)
    shift_y = jnp.clip(span_base + jitter[0], -DYM, DYM)
    shift_z = jnp.clip(deep_base + jitter[1], -DZM, DZM)
    shift_x = jnp.clip(along_base + jitter[2], -DXM, DXM)
    return jnp.stack([shift_y, shift_z, shift_x]).astype(jnp.int32)


def window_plan(key):
    base = jax.random.fold_in(key, 4051)
    devices = WINDOWS // WIN_DEV
    tile_rows = CY // STRIDE
    lower_count = 2 * GZX
    upper_count = 3 * GZX
    keys = jax.random.split(base, 3)
    lower_scores = jax.random.randint(keys[0], (devices, lower_count), 0, 4096, dtype=jnp.int32) * lower_count
    lower_scores = lower_scores + jnp.arange(lower_count, dtype=jnp.int32)[None, :]
    lower_pick = jnp.argsort(lower_scores, axis=1)[:, :CAP].astype(jnp.int32)
    upper_scores = jax.random.randint(keys[1], (devices, upper_count), 0, 4096, dtype=jnp.int32) * upper_count
    upper_scores = upper_scores + jnp.arange(upper_count, dtype=jnp.int32)[None, :]
    upper_pick = jnp.argsort(upper_scores, axis=1)[:, :WIN_DEV - CAP].astype(jnp.int32) + lower_count
    chosen = jnp.concatenate([lower_pick, upper_pick], axis=1)
    order_scores = jax.random.randint(keys[2], (devices, WIN_DEV), 0, 4096, dtype=jnp.int32) * WIN_DEV
    order_scores = order_scores + jnp.arange(WIN_DEV, dtype=jnp.int32)[None, :]
    order = jnp.argsort(order_scores, axis=1).astype(jnp.int32)
    chosen = jnp.take_along_axis(chosen, order, axis=1)
    device_ids = jnp.arange(devices, dtype=jnp.int32)[:, None]
    nodes = (device_ids * tile_rows * GZX + chosen).reshape(-1)
    field = field_plan(key).reshape(3, -1)
    return (nodes, field[:, nodes])


def draw_windows(key, part):
    return window_plan(key)[0]


def draw_shifts(key, part):
    return window_plan(key)[1]


def lattice(key):
    margin_y = DYM + 1
    margin_z = DZM + 1
    margin_x = DXM + 1
    base = jax.random.fold_in(key, 7919)
    coarse = (GY + 6, GZ + 6, GX + 6)
    level = jax.random.uniform(base, coarse, jnp.float32, 0.0, jnp.log(10.0))
    cells = jnp.exp(level)
    cells = jnp.repeat(jnp.repeat(jnp.repeat(cells, STRIDE, 0), STRIDE, 1), STRIDE, 2)
    cells = cells[3 * STRIDE - margin_y:3 * STRIDE + NY + margin_y, 3 * STRIDE - margin_z:3 * STRIDE + NZ + margin_z, 3 * STRIDE - margin_x:3 * STRIDE + NX + margin_x]
    noise = jax.random.uniform(jax.random.fold_in(key, 1), cells.shape, jnp.float32)
    return (cells * noise, cells)


def draw_first_exposure(key, part):
    margin_y = DYM + 1
    margin_z = DZM + 1
    margin_x = DXM + 1
    field, cells = lattice(key)
    return field[margin_y:margin_y + NY, margin_z:margin_z + NZ, margin_x:margin_x + NX].astype(jnp.bfloat16)


def draw_second_exposure(key, part):
    margin_y = DYM + 1
    margin_z = DZM + 1
    margin_x = DXM + 1
    field, cells = lattice(key)
    whole_shift = field_plan(key)
    residual = jax.random.uniform(jax.random.fold_in(key, 5), (3, GY, GZ, GX), jnp.float32)
    slab_shape = (STRIDE + 2 * margin_y, NZ + 2 * margin_z, NX + 2 * margin_x)

    def one_row(row):
        slab = lax.dynamic_slice(field, (row * STRIDE, 0, 0), slab_shape)
        row_shift = jnp.repeat(jnp.repeat(whole_shift[:, row], STRIDE, 1), STRIDE, 2)
        row_rest = jnp.repeat(jnp.repeat(residual[:, row], STRIDE, 1), STRIDE, 2)
        span_idx = jnp.arange(STRIDE, dtype=jnp.int32)[:, None, None] + margin_y - row_shift[0][None]
        deep_idx = jnp.arange(NZ, dtype=jnp.int32)[None, :, None] + margin_z - row_shift[1][None]
        along_idx = jnp.arange(NX, dtype=jnp.int32)[None, None, :] + margin_x - row_shift[2][None]
        span_idx = jnp.broadcast_to(span_idx, (STRIDE, NZ, NX))
        deep_idx = jnp.broadcast_to(deep_idx, (STRIDE, NZ, NX))
        along_idx = jnp.broadcast_to(along_idx, (STRIDE, NZ, NX))
        rest_y = row_rest[0][None]
        rest_z = row_rest[1][None]
        rest_x = row_rest[2][None]
        total = jnp.zeros((STRIDE, NZ, NX), jnp.float32)
        for corner_y in range(2):
            weight_y = rest_y if corner_y == 0 else 1.0 - rest_y
            for corner_z in range(2):
                weight_z = rest_z if corner_z == 0 else 1.0 - rest_z
                for corner_x in range(2):
                    weight_x = rest_x if corner_x == 0 else 1.0 - rest_x
                    picked = slab[span_idx - 1 + corner_y, deep_idx - 1 + corner_z, along_idx - 1 + corner_x]
                    total = total + weight_y * weight_z * weight_x * picked
        return total
    rows = lax.map(one_row, jnp.arange(GY, dtype=jnp.int32)).reshape(NY, NZ, NX)
    inner_cells = cells[margin_y:margin_y + NY, margin_z:margin_z + NZ, margin_x:margin_x + NX]
    fresh = jax.random.uniform(jax.random.fold_in(key, 3), (NY, NZ, NX), jnp.float32)
    return (0.9 * rows + 0.1 * inner_cells * fresh).astype(jnp.bfloat16)


def setup_inputs(seed: int = 0, part: int = 0) -> dict:
    key_of = jax.random.split(jax.random.key(seed), 5)
    own_keys = jax.random.split(jax.random.fold_in(key_of[4], part), 5)
    first_exposure = draw_first_exposure(jax.random.fold_in(jax.random.fold_in(key_of[4], part), 71), part)
    second_exposure = draw_second_exposure(jax.random.fold_in(jax.random.fold_in(key_of[4], part), 71), part)
    windows = draw_windows(jax.random.fold_in(jax.random.fold_in(key_of[4], part), 71), part)
    shifts = draw_shifts(jax.random.fold_in(jax.random.fold_in(key_of[4], part), 71), part)
    return {"first_exposure": first_exposure, "second_exposure": second_exposure, "windows": windows, "shifts": shifts}


SHARP = 80.0
EPSILON = 1e-06

def window_terms(first_pad, second_pad, node, shift):
    half_width = W // 2
    node_row = node // GZX
    node_rest = node % GZX
    node_deep = node_rest // GX
    node_along = node_rest % GX
    centre_y = STRIDE * node_row + STRIDE // 2
    centre_z = STRIDE * node_deep + STRIDE // 2
    centre_x = STRIDE * node_along + STRIDE // 2
    first_window = lax.dynamic_slice(first_pad, (centre_y, centre_z, centre_x), (W, W, W))
    pad_y = 3 * CY
    pad_z = half_width + 1 + DZM
    pad_x = half_width + 1 + DXM
    start_y = (centre_y + shift[0] - half_width - 1 + pad_y).astype(jnp.int32)
    start_z = (centre_z + shift[1] - half_width - 1 + pad_z).astype(jnp.int32)
    start_x = (centre_x + shift[2] - half_width - 1 + pad_x).astype(jnp.int32)
    second_block = lax.dynamic_slice(second_pad, (start_y, start_z, start_x), (W + 2, W + 2, W + 2))
    first_wide = first_window.astype(jnp.float32)
    first_centred = (first_wide - jnp.mean(first_wide)).astype(jnp.bfloat16)
    second_wide = second_block.astype(jnp.float32)
    second_centred = (second_wide - jnp.mean(second_wide)).astype(jnp.bfloat16)
    first_back = first_centred.astype(jnp.float32)
    second_back = second_centred.astype(jnp.float32)
    energy_first = jnp.mean(first_back * first_back)
    energy_second = jnp.mean(second_back * second_back)
    normaliser = float(W) ** 3 * jnp.sqrt((energy_first + EPSILON) * (energy_second + EPSILON))
    collected = []
    for lag_y in range(3):
        for lag_z in range(3):
            for lag_x in range(3):
                shifted_piece = lax.slice(second_back, (lag_y, lag_z, lag_x), (lag_y + W, lag_z + W, lag_x + W))
                collected.append(jnp.sum(first_back * shifted_piece))
    coherence = jnp.stack(collected).reshape(3, 3, 3) / normaliser
    weights = jnp.exp(SHARP * coherence)
    weight_sum = jnp.sum(weights)
    lag_values = jnp.array([-1.0, 0.0, 1.0], jnp.float32)
    along_y = jnp.sum(weights * lag_values[:, None, None]) / weight_sum
    along_z = jnp.sum(weights * lag_values[None, :, None]) / weight_sum
    along_x = jnp.sum(weights * lag_values[None, None, :]) / weight_sum
    return jnp.stack([along_y, along_z, along_x])

def reference(first_exposure, second_exposure, windows, shifts):
    half_width = W // 2
    first_pad = jnp.pad(first_exposure, half_width)
    pad_z = half_width + 1 + DZM
    pad_x = half_width + 1 + DXM
    second_pad = jnp.pad(second_exposure, ((3 * CY, 3 * CY), (pad_z, pad_z), (pad_x, pad_x)))

    def one_window(window_item):
        return window_terms(first_pad, second_pad, window_item[0], window_item[1])
    corrections = lax.map(one_window, (windows, shifts.T))
    update = jnp.zeros((3, GY * GZX), jnp.float32).at[:, windows].set(corrections.T)
    field_grid = update.reshape(3, GY, GZ, GX)
    padded = jnp.pad(field_grid, ((0, 0), (1, 1), (1, 1), (1, 1)))
    neighbours = padded[:, 2:, 1:-1, 1:-1] + padded[:, :-2, 1:-1, 1:-1]
    neighbours = neighbours + padded[:, 1:-1, 2:, 1:-1] + padded[:, 1:-1, :-2, 1:-1]
    neighbours = neighbours + padded[:, 1:-1, 1:-1, 2:] + padded[:, 1:-1, 1:-1, :-2]
    smoothed = 0.4 * field_grid + 0.1 * neighbours
    return smoothed.reshape(3, GY, GZX)
```

```python
import jax
import jax.numpy as jnp
from jax import lax
from jax.experimental import pallas as pl
from jax.experimental.pallas import tpu as pltpu
from jax.sharding import PartitionSpec as P

W = 48
STRIDE = 12
CY = 60
DYM = 3
GZ = 8
GX = 16
GZX = 128
HALO = DYM + 1
HALF = W // 2
BW = W + 2

SHARP = 80.0
EPSILON = 1e-06

F32 = jnp.float32
BF16 = jnp.bfloat16

OFF_Y = 24
PLANES = 112
PAD_Z = 32
ZA = 64
ZB = 80
ZA_ALL = 160
ZB_ALL = 176
GROUP = 8


def correlate_kernel(
    info, where_ref, a_hbm, b_hbm, low_hbm, high_hbm, out, a_s, b_s, b_p, gram, p_a, p_b, sems
):
    nz, nx = a_hbm.shape[1], a_hbm.shape[2]
    z_in = pl.ds(PAD_Z, nz)
    copies = [
        pltpu.make_async_copy(a_hbm, a_s.at[pl.ds(OFF_Y, CY), z_in], sems.at[0]),
        pltpu.make_async_copy(b_hbm, b_s.at[pl.ds(OFF_Y, CY), z_in], sems.at[1]),
        pltpu.make_async_copy(low_hbm, b_s.at[pl.ds(OFF_Y - HALO, HALO), z_in], sems.at[2]),
        pltpu.make_async_copy(high_hbm, b_s.at[pl.ds(OFF_Y + CY, HALO), z_in], sems.at[3]),
    ]
    for copy in copies:
        copy.start()

    def zero(ref, start, count, z_all):
        def whole(y, _):
            ref[y] = jnp.zeros((z_all, nx), BF16)
            return 0

        lax.fori_loop(0, start, whole, 0)
        lax.fori_loop(start + count, PLANES, whole, 0)

        def margins(y, _):
            ref[y, :PAD_Z] = jnp.zeros((PAD_Z, nx), BF16)
            ref[y, PAD_Z + nz :] = jnp.zeros((z_all - PAD_Z - nz, nx), BF16)
            return 0

        lax.fori_loop(start, start + count, margins, 0)

    zero(a_s, OFF_Y, CY, ZA_ALL)
    zero(b_s, OFF_Y - HALO, CY + 2 * HALO, ZB_ALL)
    out[...] = jnp.zeros_like(out)
    device = where_ref[0]
    last = where_ref[1]
    for copy in copies:
        copy.wait()

    def one_window(w, _):
        node = info[0, w]
        dy, dz, dx = info[1, w], info[2, w], info[3, w]
        side = w // 8 - 1
        present = jnp.logical_and(device + side >= 0, device + side <= last)
        cy = STRIDE * (node // GZX) + STRIDE // 2 - CY * device
        cz = STRIDE * ((node % GZX) // GX) + STRIDE // 2
        cx = STRIDE * (node % GX) + STRIDE // 2
        y_low = jnp.where(device == 0, -HALF, 0)
        y_high = jnp.where(device == last, CY + HALF, CY)
        ya = jnp.maximum(cy - HALF, y_low)
        yb = jnp.minimum(cy + HALF, y_high)
        ny = jnp.where(present, yb - ya, 0)

        @pl.when(ny > 0)
        def _():
            ta = ya - (cy - HALF)
            tb = yb - (cy - HALF)
            groups = (ny + GROUP - 1) // GROUP
            za = cz - HALF + PAD_Z
            zb = cz + dz - HALF - 1 + PAD_Z
            za0 = pl.multiple_of(za // 16 * 16, 16)
            zb0 = pl.multiple_of(zb // 16 * 16, 16)
            off_a, off_b = za - za0, zb - zb0
            xa = cx - HALF
            xb = cx + dx - HALF - 1
            a_row0 = ya + OFF_Y
            b_row0 = ya + dy - 1 + OFF_Y

            row_a = lax.broadcasted_iota(jnp.int32, (ZA, nx), 0)
            lane_a = lax.broadcasted_iota(jnp.int32, (ZA, nx), 1)
            row_b = lax.broadcasted_iota(jnp.int32, (ZB, nx), 0)
            lane_b = lax.broadcasted_iota(jnp.int32, (ZB, nx), 1)
            z_ok = (row_a >= off_a) & (row_a < off_a + W)
            plane = a_s[a_row0 + ny // 2, pl.ds(za0, ZA), :].astype(F32)
            plane = jnp.where(z_ok & (lane_a >= xa) & (lane_a < xa + W), plane, 0.0)
            pivot_a = (jnp.sum(plane, keepdims=True) * (1.0 / (W * W))).astype(BF16)
            plane = b_s[b_row0 + 1 + ny // 2, pl.ds(zb0, ZB), :].astype(F32)
            inside = (row_b >= off_b) & (row_b < off_b + BW)
            plane = jnp.where(inside & (lane_b >= xb) & (lane_b < xb + BW), plane, 0.0)
            pivot_b = (jnp.sum(plane, keepdims=True) * (1.0 / (BW * BW))).astype(BF16)
            pa32, pb32 = pivot_a.astype(F32), pivot_b.astype(F32)

            x_in = lax.broadcasted_iota(jnp.int32, (nx, 128), 0)
            lane = lax.broadcasted_iota(jnp.int32, (nx, 128), 1)
            for e in range(3):
                t = lane - e
                hit = (x_in == xa + t) & (t >= 0) & (t < W)
                p_a[:, e * 128 : (e + 1) * 128] = jnp.where(hit, 1.0, 0.0).astype(BF16)
            hit = (x_in == xb + lane) & (lane < BW)
            p_b[...] = jnp.where(hit, 1.0, 0.0).astype(BF16)

            z_keep = jnp.where(z_ok, 1.0, 0.0).astype(BF16)
            ones_row = jnp.where(row_a == ZA - 1, 1.0, 0.0).astype(BF16)
            row_e = lax.broadcasted_iota(jnp.int32, (ZA, 128), 0)
            lane_e = lax.broadcasted_iota(jnp.int32, (ZA, 128), 1)
            beyond = jnp.where(
                row_e == ZA - 1,
                1.0,
                jnp.where((row_e >= off_a) & (row_e < off_a + W), -pa32, 0.0),
            )
            edge_a = []
            for e in range(3):
                t = lane_e - e
                outside = (t >= 0) & (t < W) & ((xa + t < 0) | (xa + t >= nx))
                edge_a.append(jnp.where(outside, beyond, 0.0))
            lane_q = lax.broadcasted_iota(jnp.int32, (1, ZB, 128), 2)
            outside = (lane_q < BW) & ((xb + lane_q < 0) | (xb + lane_q >= nx))
            edge_b = jnp.where(outside, jnp.broadcast_to(-pb32[None], (1, ZB, 128)), 0.0)

            q_low = jnp.where(ta == 0, 0, 1)
            q_high = jnp.where(tb == W, ny + 2, ny + 1)
            row_q = lax.broadcasted_iota(jnp.int32, (ZB, 128), 0)
            z_in_block = (row_q >= off_b) & (row_q < off_b + BW)

            def second_rows(g, carry):
                sum_b, sum_bb = carry
                x = b_s[pl.ds(b_row0 + g * GROUP, GROUP), pl.ds(zb0, ZB), :] - pivot_b[None]
                t = jnp.dot(
                    x.reshape(GROUP * ZB, nx), p_b[...], preferred_element_type=F32
                ).reshape(GROUP, ZB, 128)
                t = t + edge_b
                b_p[pl.ds(g * GROUP, GROUP)] = t.astype(BF16)
                for i in range(GROUP):
                    q = g * GROUP + i
                    keep = jnp.where((q >= q_low) & (q < q_high), 1.0, 0.0)
                    v = t[i] * keep
                    sum_b = sum_b + v
                    sum_bb = sum_bb + v * v
                return sum_b, sum_bb

            zeros = jnp.zeros((ZB, 128), F32)
            sum_b, sum_bb = lax.fori_loop(0, groups + 1, second_rows, (zeros, zeros))
            gram[...] = jnp.zeros_like(gram)

            def first_rows(g, carry):
                sum_a, sum_aa = carry
                x = a_s[pl.ds(a_row0 + g * GROUP, GROUP), pl.ds(za0, ZA), :]
                x = (x - pivot_a[None]) * z_keep[None] + ones_row[None]
                t = jnp.dot(x.reshape(GROUP * ZA, nx), p_a[...], preferred_element_type=F32)
                left, right = [], []
                for i in range(GROUP):
                    keep = jnp.where(g * GROUP + i < ny, 1.0, 0.0)
                    pieces = []
                    for e in range(3):
                        v = t[i * ZA : (i + 1) * ZA, e * 128 : (e + 1) * 128]
                        v = (v + edge_a[e]) * keep
                        if e == 0:
                            sum_a = sum_a + v
                            sum_aa = sum_aa + v * v
                        pieces.append(v.astype(BF16))
                    left.append(jnp.concatenate(pieces, axis=0))
                    right.append(b_p[pl.ds(g * GROUP + i, 3)].reshape(3 * ZB, 128))
                gram[...] += lax.dot_general(
                    jnp.concatenate(left, axis=1),
                    jnp.concatenate(right, axis=1),
                    (((1,), (1,)), ((), ())),
                    preferred_element_type=F32,
                )
                return sum_a, sum_aa

            zeros_a = jnp.zeros((ZA, 128), F32)
            sum_a, sum_aa = lax.fori_loop(0, groups, first_rows, (zeros_a, zeros_a))

            row_g = lax.broadcasted_iota(jnp.int32, (ZA, 3 * ZB), 0)
            col_g = lax.broadcasted_iota(jnp.int32, (ZA, 3 * ZB), 1)
            seg = jnp.where(col_g >= 2 * ZB, 2, jnp.where(col_g >= ZB, 1, 0))
            q_g = col_g - ZB * seg
            gap = q_g - row_g - (off_b - off_a)
            real = row_g < ZA - 1
            lines = []
            for f in range(3):
                for e in range(3):
                    block = gram[e * ZA : (e + 1) * ZA, :]
                    lines.append(
                        jnp.sum(jnp.where(real & (gap == f), block, 0.0), axis=0, keepdims=True)
                    )
            q_1 = q_g[:1]
            for f in range(3):
                span = (q_1 >= off_b + f) & (q_1 < off_b + f + W)
                for e in range(3):
                    line = gram[(e + 1) * ZA - 1 : (e + 1) * ZA, :]
                    lines.append(jnp.where(span, line, 0.0))
            lines.append(jnp.zeros((6, 3 * ZB), F32))
            stack = jnp.concatenate(lines, axis=0)
            seg_s = lax.broadcasted_iota(jnp.int32, (24, 3 * ZB), 1)
            here = lax.broadcasted_iota(jnp.int32, (24, 128), 1) == w
            for s in range(3):
                inside = (seg_s >= s * ZB) & (seg_s < (s + 1) * ZB)
                total = jnp.sum(jnp.where(inside, stack, 0.0), axis=1, keepdims=True)
                out[s * 24 : (s + 1) * 24, :] += jnp.where(here, total, 0.0)

            real_e = row_e < ZA - 1
            row_8 = lax.broadcasted_iota(jnp.int32, (8, 128), 0)
            stats = (
                jnp.sum(jnp.where(real_e, sum_a, 0.0), keepdims=True),
                jnp.sum(jnp.where(real_e, sum_aa, 0.0), keepdims=True),
                jnp.sum(jnp.where(z_in_block, sum_b, 0.0), keepdims=True),
                jnp.sum(jnp.where(z_in_block, sum_bb, 0.0), keepdims=True),
                pa32,
                pb32,
                jnp.full((1, 1), (ny * (W * W)).astype(F32)),
                jnp.full((1, 1), ((q_high - q_low) * (BW * BW)).astype(F32)),
            )
            rows = jnp.zeros((8, 128), F32)
            for r, value in enumerate(stats):
                rows = jnp.where(row_8 == r, value, rows)
            out[72:80, :] += jnp.where(here[:8], rows, 0.0)

        return 0

    lax.fori_loop(0, 24, one_window, 0)


def finish_kernel(info, where_ref, mine, low, high, out):
    parts = (mine[...], pltpu.roll(low[...], 120, 1), pltpu.roll(high[...], 8, 1))
    stats = [[p[72 + r : 73 + r] for r in range(8)] for p in parts]
    mean_a = sum(s[0] + s[6] * s[4] for s in stats) / float(W) ** 3
    mean_b = sum(s[2] + s[7] * s[5] for s in stats) / float(BW) ** 3
    energy_a = jnp.zeros((1, 128), F32)
    energy_b = jnp.zeros((1, 128), F32)
    corr = [jnp.zeros((9, 128), F32) for _ in range(3)]
    for p, s in zip(parts, stats):
        da = s[4] - mean_a
        db = s[5] - mean_b
        energy_a += s[1] + 2.0 * da * s[0] + s[6] * da * da
        energy_b += s[3] + 2.0 * db * s[2] + s[7] * db * db
        rest = db * s[0] + s[6] * da * db
        for y in range(3):
            base = 24 * y
            corr[y] = corr[y] + (p[base : base + 9] + da * p[base + 9 : base + 18] + rest)
    energy_a = energy_a / float(W) ** 3
    energy_b = energy_b / float(BW) ** 3
    normaliser = float(W) ** 3 * jnp.sqrt((energy_a + EPSILON) * (energy_b + EPSILON))
    weights = [jnp.exp(SHARP * (c / normaliser)) for c in corr]
    sums = [jnp.sum(v, axis=0, keepdims=True) for v in weights]
    total = sums[0] + sums[1] + sums[2]
    every = weights[0] + weights[1] + weights[2]
    row_9 = lax.broadcasted_iota(jnp.int32, (9, 128), 0)
    lag_z = jnp.where(row_9 >= 6, 1.0, jnp.where(row_9 >= 3, 0.0, -1.0))
    row_x = row_9 - jnp.where(row_9 >= 6, 6, jnp.where(row_9 >= 3, 3, 0))
    lag_x = row_x.astype(F32) - 1.0
    along = (
        (sums[2] - sums[0]) / total,
        jnp.sum(every * lag_z, axis=0, keepdims=True) / total,
        jnp.sum(every * lag_x, axis=0, keepdims=True) / total,
    )
    device = where_ref[0]
    last = where_ref[1]
    row = lax.broadcasted_iota(jnp.int32, (8, GZX), 0)
    lane = lax.broadcasted_iota(jnp.int32, (8, GZX), 1)
    fields = [jnp.zeros((8, GZX), F32) for _ in range(3)]
    rows_tile = CY // STRIDE
    for w in range(24):
        side = w // 8 - 1
        present = jnp.logical_and(device + side >= 0, device + side <= last)
        node = info[0, w]
        at_row = jnp.where(present, node // GZX - rows_tile * device + 1, -1)
        at = (row == at_row) & (lane == node % GZX)
        for c in range(3):
            fields[c] = jnp.where(at, along[c][:, w : w + 1], fields[c])
    deep = lane // GX
    stream = lane % GX
    for c in range(3):
        u = fields[c]
        near = (
            jnp.where(deep < GZ - 1, pltpu.roll(u, GZX - GX, 1), 0.0)
            + jnp.where(deep > 0, pltpu.roll(u, GX, 1), 0.0)
            + jnp.where(stream < GX - 1, pltpu.roll(u, GZX - 1, 1), 0.0)
            + jnp.where(stream > 0, pltpu.roll(u, 1, 1), 0.0)
        )
        near = near + pltpu.roll(u, 7, 0) + pltpu.roll(u, 1, 0)
        out[c] = (0.4 * u + 0.1 * near)[1 : 1 + rows_tile]


def shards(first_exposure, second_exposure, windows, shifts):
    count = lax.axis_size("span")
    device = lax.axis_index("span")
    forward = [(i, i + 1) for i in range(count - 1)]
    backward = [(i + 1, i) for i in range(count - 1)]
    nz, nx = first_exposure.shape[1:]
    info = jnp.concatenate([windows[None], shifts], axis=0)
    info_low = lax.ppermute(info, "span", forward)
    info_high = lax.ppermute(info, "span", backward)
    low = lax.ppermute(second_exposure[CY - HALO :], "span", forward)
    high = lax.ppermute(second_exposure[:HALO], "span", backward)
    info = jnp.concatenate([info_low, info, info_high], axis=1)
    where_am = jnp.stack([device, jnp.int32(count - 1)]).astype(jnp.int32)
    smem = pl.BlockSpec(memory_space=pltpu.SMEM)
    hbm = pl.BlockSpec(memory_space=pl.ANY)
    vmem = pl.BlockSpec(memory_space=pltpu.VMEM)
    mine = pl.pallas_call(
        correlate_kernel,
        out_shape=jax.ShapeDtypeStruct((80, 128), F32),
        in_specs=[smem, smem, hbm, hbm, hbm, hbm],
        out_specs=vmem,
        scratch_shapes=[
            pltpu.VMEM((PLANES, ZA_ALL, nx), BF16),
            pltpu.VMEM((PLANES, ZB_ALL, nx), BF16),
            pltpu.VMEM((64, ZB, 128), BF16),
            pltpu.VMEM((3 * ZA, 3 * ZB), F32),
            pltpu.VMEM((nx, 384), BF16),
            pltpu.VMEM((nx, 128), BF16),
            pltpu.SemaphoreType.DMA((4,)),
        ],
        compiler_params=pltpu.CompilerParams(vmem_limit_bytes=48 << 20),
    )(info, where_am, first_exposure, second_exposure, low, high)
    from_low = lax.ppermute(mine, "span", forward)
    from_high = lax.ppermute(mine, "span", backward)
    return pl.pallas_call(
        finish_kernel,
        out_shape=jax.ShapeDtypeStruct((3, CY // STRIDE, GZX), F32),
        in_specs=[smem, smem, vmem, vmem, vmem],
        out_specs=vmem,
    )(info, where_am, mine, from_low, from_high)


def solution(mesh):
    in_specs = (
        P(("grp", "span"), None, None),
        P(("grp", "span"), None, None),
        P(("grp", "span")),
        P(None, ("grp", "span")),
    )
    out_specs = P(None, ("grp", "span"), None)
    return jax.shard_map(shards, mesh=mesh, in_specs=in_specs, out_specs=out_specs, check_vma=False)
```
